32 devices in a mesh: vocab: 8 (over z, x), tok: 4 (over y, core).
Axes of the slice: x: 2, y: 2, z: 4, core: 2. Of those that a mesh axis runs over, the one named last changes fastest.
Arguments:
- src_embed: bfloat16 [8192, 8192], P('vocab', 'tok'), may hold values from -6 to 6
- src_head: bfloat16 [8192, 8192], P('vocab', 'tok'), may hold values from -0.25 to 0.25
- block_ids: int32 [64, 3], P('vocab'), may hold values from 0 to 63, as said below
- slot_counts: int32 [64], P('vocab'), may hold values from 1 to 3
- slot_weights: bfloat16 [64, 3, 128, 128], P('vocab'), may hold values from -0.375 to 0.375
- hidden: bfloat16 [2048, 8192], P('tok', 'vocab'), may hold values from -48 to 48
- targets: int32 [2048], P('tok'), may hold values from 0 to 8191
- byte_counts: int32 [2048], P('tok'), may hold values from 1 to 8
Outputs:
- new_embed: bfloat16 [8192, 8192], P('vocab', 'tok')
- token_bpb: float32 [2048], P('tok')
The draws below stay inside these ranges and needn't reach their ends.
Inputs may be any that keep to these rules, and one draw needn't show every extreme that they name: `block_ids`: slot k of new block b names a source block between b - 2 and b + 2.
All inputs are finite; a program needn't handle non-finite values.
Results may differ from the reference program's by a relative error of at most 0.005.
Values may be sent and summed in bfloat16 or wider, within the bound.
No kernel may reach another device: no remote copies, remote signals or barrier semaphores. Data moves between devices by JAX's collectives and lax.ppermute only.
A program may use at most 128 MiB of HBM per device.

```python
import math
import jax
import jax.numpy as jnp
import numpy as np
from jax import lax

D = 8192
BLOCK = 128
SLOTS = 3
REACH = 2
VS = 8192
NV = 8192
NBLK = 64
TOKENS = 2048


def draw_block_ids(key, part):
    count_blocks = NV // BLOCK
    anchor = jnp.arange(count_blocks, dtype=jnp.int32)[:, None]
    offsets = jax.random.randint(key, (count_blocks, SLOTS), -REACH, REACH + 1, dtype=jnp.int32)
    return jnp.clip(anchor + offsets, 0, VS // BLOCK - 1).astype(jnp.int32)


def draw_hidden(key, part):
    first = jax.random.fold_in(key, 0)
    values = jnp.clip(jax.random.normal(first, (TOKENS, D), jnp.float32), -6.0, 6.0)
    return values.astype(jnp.bfloat16)


def set_ends(entries, stream_key, least, largest):
    index_at = [jax.random.randint(jax.random.fold_in(stream_key, axis), (), 0, length) for axis, length in enumerate(entries.shape)]
    main_axis = entries.shape.index(max(entries.shape))
    neighbour = index_at[:main_axis] + [(index_at[main_axis] + 1) % entries.shape[main_axis]] + index_at[main_axis + 1:]
    return entries.at[tuple(index_at)].set(least).at[tuple(neighbour)].set(largest)


def level_of(rng, extent, cuts, least, high):
    factor_of, own = 1.0, jax.random.fold_in(rng, 6)
    for axis_at, blocks in cuts:
        draws = jnp.exp(jax.random.uniform(jax.random.fold_in(own, axis_at), (blocks,), jnp.float32, least / len(cuts), high / len(cuts)))
        factor_of = factor_of * jnp.repeat(draws, extent[axis_at] // blocks).reshape([-1 if axis == axis_at else 1 for axis in range(len(extent))])
    return factor_of


def rank_bounds(count, lean):
    portions = [(1 << 20) // math.isqrt(standing ** lean) + 1 for standing in range(1, count + 1)]
    spread = 1 + sum(portions) // (1 << 30)
    return np.cumsum(np.array([max(1, weight // spread) for weight in portions]))


def ranked_ids(key, dims, number_of, lean):
    table = rank_bounds(number_of, lean)
    lot = jax.random.randint(jax.random.fold_in(key, 1), dims, 0, int(table[number_of - 1]))
    rank = jnp.searchsorted(jnp.asarray(table, jnp.int32), lot, side="right")
    return jax.random.permutation(jax.random.fold_in(key, 2), number_of)[rank].astype(jnp.int32)


def bell_draw(key, extent, deviation, limit, cuts=(), held_as=jnp.bfloat16):
    values = jax.random.normal(key, extent, jnp.float32) * deviation
    if len(cuts) > 0:
        values = level_of(key, extent, cuts, -0.22, 0.18) * values
    return jnp.clip(values, min=-limit, max=limit).astype(held_as)


def setup_inputs(seed: int = 0) -> dict:
    keys = jax.random.split(jax.random.key(seed), 9)
    src_embed = bell_draw(keys[0], (VS, D), 1.0, 6.0, ((0, 8), (1, 4)))
    src_head = bell_draw(keys[1], (VS, D), (D // 16) ** -0.5, 0.25, ((0, 8), (1, 4)))
    block_ids = draw_block_ids(jax.random.fold_in(keys[8], 71), 0)
    slot_counts = set_ends(jax.random.randint(keys[3], (NBLK,), 1, SLOTS + 1), jax.random.fold_in(keys[3], 1), 1, SLOTS).astype(jnp.int32)
    slot_weights = bell_draw(keys[4], (NBLK, SLOTS, BLOCK, BLOCK), (BLOCK * 2) ** -0.5, 0.375, ((0, 8),))
    hidden = draw_hidden(jax.random.fold_in(keys[8], 71), 0)
    targets = set_ends(ranked_ids(keys[6], (TOKENS,), NV, 2), jax.random.fold_in(keys[6], 3), 0, NV - 1).astype(jnp.int32)
    byte_counts = set_ends(jax.random.randint(keys[7], (TOKENS,), 1, 9), jax.random.fold_in(keys[7], 1), 1, 8).astype(jnp.int32)
    return dict(src_embed=src_embed, src_head=src_head, block_ids=block_ids, slot_counts=slot_counts, slot_weights=slot_weights, hidden=hidden, targets=targets, byte_counts=byte_counts)


def blend(table, block_ids, slot_counts, slot_weights):
    width = table.shape[1]
    blocks = table.reshape(-1, BLOCK, width)

    def one_block(items):
        names, amount, weights = items
        summed = jnp.zeros((BLOCK, width), jnp.float32)
        for slot in range(SLOTS):
            rows = lax.dynamic_index_in_dim(blocks, names[slot], 0, keepdims=False)
            masked = jnp.where(slot < amount, weights[slot], jnp.zeros_like(weights[slot]))
            summed = summed + jnp.dot(masked, rows, preferred_element_type=jnp.float32)
        return summed.astype(jnp.bfloat16)

    result = lax.map(one_block, (block_ids, slot_counts, slot_weights))
    return result.reshape(-1, width)


def reference(src_embed, src_head, block_ids, slot_counts, slot_weights, hidden, targets, byte_counts):
    new_embed = blend(src_embed, block_ids, slot_counts, slot_weights)
    new_head = blend(src_head, block_ids, slot_counts, slot_weights)
    stride = math.gcd(TOKENS, 128)

    def score(items):
        rows, goals, nbytes = items
        logits = lax.dot_general(rows, new_head, (((1,), (1,)), ((), ())), preferred_element_type=jnp.float32)
        peak = jnp.max(logits, axis=1)
        log_total = peak + jnp.log(jnp.sum(jnp.exp(logits - peak[:, None]), axis=1))
        chosen = jnp.take_along_axis(logits, goals[:, None].astype(jnp.int32), axis=1)[:, 0]
        return (log_total - chosen) / (jnp.float32(math.log(2.0)) * nbytes.astype(jnp.float32))

    token_bpb = lax.map(score, (hidden.reshape(-1, stride, D), targets.reshape(-1, stride), byte_counts.reshape(-1, stride)))
    return new_embed, token_bpb.reshape(-1)
```

```python
import functools
import math

import jax
import jax.numpy as jnp
from jax import lax
from jax.experimental import pallas as pl
from jax.experimental.pallas import tpu as pltpu
from jax.sharding import PartitionSpec as P

REACH = 2


def xor_perm(count, mask):
    return [(i, i ^ mask) for i in range(count)]


def masked(weights, slot, amount):
    return jnp.where(slot < amount, weights, jnp.zeros_like(weights))


def fill_padded(padded, before_ref, own_ref, after_ref):
    edge, rows = before_ref.shape[0], own_ref.shape[0]
    padded[pl.ds(0, edge), :] = before_ref[...]
    padded[pl.ds(edge, rows), :] = own_ref[...]
    padded[pl.ds(edge + rows, edge), :] = after_ref[...]


def blend_block(ids_ref, counts_ref, weights_ref, padded, block):
    slots, rows = weights_ref.shape[1], weights_ref.shape[2]
    total = None
    for slot in range(slots):
        start = pl.multiple_of(ids_ref[block, slot] * rows, rows)
        part = jnp.dot(
            masked(weights_ref[block, slot], slot, counts_ref[block]),
            padded[pl.ds(start, rows), :],
            preferred_element_type=jnp.float32,
        )
        total = part if total is None else total + part
    return total


def table_kernel(ids_ref, counts_ref, weights_ref, before_ref, own_ref, after_ref, out_ref, padded):
    fill_padded(padded, before_ref, own_ref, after_ref)
    blocks, rows = weights_ref.shape[0], weights_ref.shape[2]
    for block in range(blocks):
        summed = blend_block(ids_ref, counts_ref, weights_ref, padded, block)
        out_ref[pl.ds(block * rows, rows), :] = summed.astype(out_ref.dtype)


def blend_table(ids, counts, weights, before, own, after, tile=512):
    rows, columns = own.shape
    edge = before.shape[0]
    tile = math.gcd(tile, columns)
    smem = pl.BlockSpec(memory_space=pltpu.SMEM)
    return pl.pallas_call(
        table_kernel,
        grid=(columns // tile,),
        out_shape=jax.ShapeDtypeStruct((weights.shape[0] * weights.shape[2], columns), own.dtype),
        in_specs=[
            smem,
            smem,
            pl.BlockSpec(weights.shape, lambda i: (0, 0, 0, 0)),
            pl.BlockSpec((edge, tile), lambda i: (0, i)),
            pl.BlockSpec((rows, tile), lambda i: (0, i)),
            pl.BlockSpec((edge, tile), lambda i: (0, i)),
        ],
        out_specs=pl.BlockSpec((weights.shape[0] * weights.shape[2], tile), lambda i: (0, i)),
        scratch_shapes=[pltpu.VMEM((rows + 2 * edge, tile), own.dtype)],
        compiler_params=pltpu.CompilerParams(vmem_limit_bytes=32 << 20),
        cost_estimate=pl.CostEstimate(
            flops=2 * weights.size * columns,
            bytes_accessed=2 * (2 * rows + 2 * edge) * columns + 2 * weights.size,
            transcendentals=0,
        ),
        name="blend_table",
    )(ids, counts, weights, before, own, after)


def stats_kernel(ids_ref, counts_ref, weights_ref, before_ref, own_ref, after_ref, goals_ref, out_ref, padded, logits):
    fill_padded(padded, before_ref, own_ref, after_ref)
    blocks, rows = weights_ref.shape[0], weights_ref.shape[2]
    tokens = own_ref.shape[1]
    goals = goals_ref[...]
    peak = jnp.full((1, tokens), -jnp.inf, jnp.float32)
    picked = jnp.zeros((1, tokens), jnp.float32)
    for block in range(blocks):
        summed = blend_block(ids_ref, counts_ref, weights_ref, padded, block)
        logits[pl.ds(block * rows, rows), :] = summed
        peak = jnp.maximum(peak, jnp.max(summed, axis=0, keepdims=True))
        row_ids = lax.broadcasted_iota(jnp.int32, summed.shape, 0) + block * rows
        picked = picked + jnp.sum(jnp.where(row_ids == goals, summed, 0.0), axis=0, keepdims=True)
    total = jnp.zeros((1, tokens), jnp.float32)
    for block in range(blocks):
        values = jnp.exp(logits[pl.ds(block * rows, rows), :] - peak)
        total = total + jnp.sum(values, axis=0, keepdims=True)
    out_ref[0:1, :] = peak
    out_ref[1:2, :] = total
    out_ref[2:3, :] = picked


def local_stats(ids, counts, weights, before, own, after, goals):
    rows, tokens = own.shape
    edge = before.shape[0]
    smem = pl.BlockSpec(memory_space=pltpu.SMEM)
    vmem = pl.BlockSpec(memory_space=pltpu.VMEM)
    new_rows = weights.shape[0] * weights.shape[2]
    return pl.pallas_call(
        stats_kernel,
        out_shape=jax.ShapeDtypeStruct((3, tokens), jnp.float32),
        in_specs=[smem, smem, vmem, vmem, vmem, vmem, vmem],
        out_specs=vmem,
        scratch_shapes=[
            pltpu.VMEM((rows + 2 * edge, tokens), own.dtype),
            pltpu.VMEM((new_rows, tokens), jnp.float32),
        ],
        compiler_params=pltpu.CompilerParams(vmem_limit_bytes=32 << 20),
        cost_estimate=pl.CostEstimate(
            flops=2 * weights.size * tokens, bytes_accessed=4 * rows * tokens, transcendentals=new_rows * tokens
        ),
        name="blend_stats",
    )(ids, counts, weights, before, own, after, goals)


def edges(value, axis, width):
    count, length = lax.axis_size(axis), value.shape[0]
    up = [(i, i + 1) for i in range(count - 1)]
    down = [(j, i) for i, j in up]
    before = lax.ppermute(lax.slice_in_dim(value, length - width, length, axis=0), axis, up)
    after = lax.ppermute(lax.slice_in_dim(value, 0, width, axis=0), axis, down)
    return before, after


def merge_stats(stats, axis):
    count = lax.axis_size(axis)
    index = lax.axis_index(axis)
    mask = 1
    while mask < count:
        other = lax.ppermute(stats, axis, xor_perm(count, mask))
        upper = (index & mask) != 0
        first = jnp.where(upper, other, stats)
        second = jnp.where(upper, stats, other)
        peak = jnp.maximum(first[0], second[0])
        total = first[1] * jnp.exp(first[0] - peak) + second[1] * jnp.exp(second[0] - peak)
        stats = jnp.stack([peak, total, first[2] + second[2]])
        mask *= 2
    return stats


def body(src_embed, src_head, block_ids, slot_counts, slot_weights, hidden, targets, byte_counts):
    block_rows = slot_weights.shape[2]
    rows, quarter = src_embed.shape
    new_rows = slot_weights.shape[0] * block_rows
    vocab_index = lax.axis_index("vocab")
    tok_index = lax.axis_index("tok")
    tok_count = lax.axis_size("tok")
    halo = REACH * block_rows
    last_local = rows // block_rows + 2 * REACH - 1
    local_ids = jnp.clip(block_ids - (vocab_index * (rows // block_rows) - REACH), 0, last_local)

    whole_rows = lax.all_gather(hidden, "vocab", axis=1, tiled=True)
    pieces = {0: src_head}
    mask = tok_count // 2
    while mask >= 1:
        for held in list(pieces):
            pieces[held | mask] = lax.ppermute(pieces[held], "tok", xor_perm(tok_count, mask))
        mask //= 2

    source_logits = None
    for held, piece in pieces.items():
        columns = lax.dynamic_slice_in_dim(whole_rows, (tok_index ^ held) * quarter, quarter, axis=1)
        part = lax.dot_general(piece, columns, (((1,), (1,)), ((), ())), preferred_element_type=jnp.float32)
        source_logits = part if source_logits is None else source_logits + part
    source_logits = source_logits.astype(jnp.bfloat16)
    before, after = edges(source_logits, "vocab", halo)
    goals = (targets - vocab_index * new_rows)[None, :]
    stats = local_stats(local_ids, slot_counts, slot_weights, before, source_logits, after, goals)
    stats = merge_stats(stats, "vocab")
    log_total = stats[0] + jnp.log(stats[1])
    token_bpb = (log_total - stats[2]) / (jnp.float32(math.log(2.0)) * byte_counts.astype(jnp.float32))

    before, after = edges(src_embed, "vocab", halo)
    new_embed = blend_table(local_ids, slot_counts, slot_weights, before, src_embed, after)
    return (new_embed, token_bpb)


def solution(mesh):
    in_specs = (
        P("vocab", "tok"),
        P("vocab", "tok"),
        P("vocab", None),
        P("vocab"),
        P("vocab", None, None, None),
        P("tok", "vocab"),
        P("tok"),
        P("tok"),
    )
    out_specs = (P("vocab", "tok"), P("tok"))
    return jax.shard_map(body, mesh=mesh, in_specs=in_specs, out_specs=out_specs, check_vma=False)
```

```python
import functools
import math

import jax
import jax.numpy as jnp
from jax import lax
from jax.experimental import pallas as pl
from jax.experimental.pallas import tpu as pltpu
from jax.sharding import PartitionSpec as P

REACH = 2
CONTRACT_LAST = (((1,), (1,)), ((), ()))


def xor_perm(count, mask):
    return [(i, i ^ mask) for i in range(count)]


def masked(weights, slot, amount):
    return jnp.where(slot < amount, weights, jnp.zeros_like(weights))


def blend_block(ids_ref, counts_ref, weights_ref, padded, block):
    slots, rows = weights_ref.shape[1], weights_ref.shape[2]
    total = None
    for slot in range(slots):
        start = pl.multiple_of(ids_ref[block, slot] * rows, rows)
        part = jnp.dot(
            masked(weights_ref[block, slot], slot, counts_ref[block]),
            padded[pl.ds(start, rows), :],
            preferred_element_type=jnp.float32,
        )
        total = part if total is None else total + part
    return total


def table_kernel(ids_ref, counts_ref, side_ref, weights_ref, own_ref, before_ref, after_ref, relayed_ref, out_ref, padded):
    edge, own_rows = before_ref.shape[0], own_ref.shape[0]
    padded[pl.ds(0, edge), :] = before_ref[...]
    padded[pl.ds(edge, own_rows), :] = own_ref[...]
    padded[pl.ds(edge + own_rows, edge), :] = after_ref[...]

    @pl.when(side_ref[0] == 1)
    def _():
        padded[pl.ds(0, edge), :] = relayed_ref[...]

    @pl.when(side_ref[0] == 2)
    def _():
        padded[pl.ds(edge + own_rows, edge), :] = relayed_ref[...]

    blocks, rows = weights_ref.shape[0], weights_ref.shape[2]
    for block in range(blocks):
        summed = blend_block(ids_ref, counts_ref, weights_ref, padded, block)
        out_ref[pl.ds(block * rows, rows), :] = summed.astype(out_ref.dtype)


def blend_table(ids, counts, weights, own, before, after, relayed, side, tile=512):
    rows, columns = own.shape
    edge = before.shape[0]
    tile = math.gcd(tile, columns)
    smem = pl.BlockSpec(memory_space=pltpu.SMEM)
    strip = lambda count: pl.BlockSpec((count, tile), lambda i: (0, i))
    new_rows = weights.shape[0] * weights.shape[2]
    return pl.pallas_call(
        table_kernel,
        grid=(columns // tile,),
        out_shape=jax.ShapeDtypeStruct((new_rows, columns), own.dtype),
        in_specs=[smem, smem, smem, pl.BlockSpec(weights.shape, lambda i: (0, 0, 0, 0)), strip(rows)] + [strip(edge)] * 3,
        out_specs=strip(new_rows),
        scratch_shapes=[pltpu.VMEM((rows + 2 * edge, tile), own.dtype)],
        compiler_params=pltpu.CompilerParams(vmem_limit_bytes=32 << 20),
        cost_estimate=pl.CostEstimate(
            flops=0, bytes_accessed=0, transcendentals=0
        ),
        name="blend_table",
    )(ids, counts, side, weights, own, before, after, relayed)


def stats_kernel(ids_ref, counts_ref, weights_ref, *refs):
    *source_refs, goals_ref, out_ref, padded, logits = refs
    start = 0
    for source_ref in source_refs:
        padded[pl.ds(start, source_ref.shape[0]), :] = source_ref[...]
        start += source_ref.shape[0]
    blocks, rows = weights_ref.shape[0], weights_ref.shape[2]
    tokens = padded.shape[1]
    goals = goals_ref[...]
    peak = jnp.full((1, tokens), -jnp.inf, jnp.float32)
    picked = jnp.zeros((1, tokens), jnp.float32)
    for block in range(blocks):
        summed = blend_block(ids_ref, counts_ref, weights_ref, padded, block)
        logits[pl.ds(block * rows, rows), :] = summed
        peak = jnp.maximum(peak, jnp.max(summed, axis=0, keepdims=True))
        row_ids = lax.broadcasted_iota(jnp.int32, summed.shape, 0) + block * rows
        picked = picked + jnp.sum(jnp.where(row_ids == goals, summed, 0.0), axis=0, keepdims=True)
    total = jnp.zeros((1, tokens), jnp.float32)
    for block in range(blocks):
        values = jnp.exp(logits[pl.ds(block * rows, rows), :] - peak)
        total = total + jnp.sum(values, axis=0, keepdims=True)
    out_ref[0:1, :] = peak
    out_ref[1:2, :] = total
    out_ref[2:3, :] = picked


def local_stats(ids, counts, weights, source, goals):
    tokens = source[0].shape[1]
    source_rows = sum(value.shape[0] for value in source)
    smem = pl.BlockSpec(memory_space=pltpu.SMEM)
    vmem = pl.BlockSpec(memory_space=pltpu.VMEM)
    new_rows = weights.shape[0] * weights.shape[2]
    return pl.pallas_call(
        stats_kernel,
        out_shape=jax.ShapeDtypeStruct((3, tokens), jnp.float32),
        in_specs=[smem, smem, vmem] + [vmem] * (len(source) + 1),
        out_specs=vmem,
        scratch_shapes=[
            pltpu.VMEM((source_rows, tokens), source[0].dtype),
            pltpu.VMEM((new_rows, tokens), jnp.float32),
        ],
        compiler_params=pltpu.CompilerParams(vmem_limit_bytes=32 << 20),
        cost_estimate=pl.CostEstimate(
            flops=2 * weights.size * tokens, bytes_accessed=2 * source_rows * tokens, transcendentals=new_rows * tokens
        ),
        name="blend_stats",
    )(ids, counts, weights, *source, goals)


def product_kernel(where_ref, *refs, pieces, chunks, final):
    piece_refs, refs = refs[:pieces], refs[pieces:]
    chunk_refs, refs = refs[:chunks], refs[chunks:]
    carried_ref, refs = (refs[0], refs[1:]) if final else (None, refs)
    *out_refs, held, block, sems = refs
    width = held.shape[2]

    def column_copy(at, piece_ref):
        start = pl.multiple_of(where_ref[1, at] * width, width)
        return pltpu.make_async_copy(piece_ref.at[:, pl.ds(start, width)], held.at[at], sems.at[0, at])

    def block_copy(at):
        return pltpu.make_async_copy(chunk_refs[at], block.at[at], sems.at[1, at])

    for at in range(chunks):
        block_copy(at).start()
        for piece, piece_ref in enumerate(piece_refs):
            @pl.when(where_ref[0, at] == piece)
            def _(at=at, piece_ref=piece_ref):
                column_copy(at, piece_ref).start()

    for at in range(chunks):
        block_copy(at).wait()
        column_copy(at, piece_refs[0]).wait()
        row = 0
        for out_ref in out_refs:
            size = out_ref.shape[0]
            part = lax.dot_general(
                held[at, row : row + size, :], block[at], CONTRACT_LAST, preferred_element_type=jnp.float32
            )
            if final:
                out_ref[...] = (part + carried_ref[row : row + size, :]).astype(out_ref.dtype)
            elif at == 0:
                out_ref[...] = part
            else:
                out_ref[...] += part
            row += size


def add_products(where, pieces, chunks, carried=None, out_rows=()):
    rows, (tokens, width) = pieces[0].shape[0], chunks[0].shape
    final = carried is not None
    vmem = pl.BlockSpec(memory_space=pltpu.VMEM)
    hbm = pl.BlockSpec(memory_space=pltpu.HBM)
    shapes = [(size, tokens) for size in out_rows] if final else [(rows, tokens)]
    return pl.pallas_call(
        functools.partial(product_kernel, pieces=len(pieces), chunks=len(chunks), final=final),
        out_shape=[jax.ShapeDtypeStruct(shape, jnp.bfloat16 if final else jnp.float32) for shape in shapes],
        in_specs=[pl.BlockSpec(memory_space=pltpu.SMEM)] + [hbm] * (len(pieces) + len(chunks)) + [vmem] * final,
        out_specs=[vmem] * len(shapes),
        scratch_shapes=[
            pltpu.VMEM((len(chunks), rows, width), jnp.bfloat16),
            pltpu.VMEM((len(chunks), tokens, width), jnp.bfloat16),
            pltpu.SemaphoreType.DMA((2, len(chunks))),
        ],
        compiler_params=pltpu.CompilerParams(vmem_limit_bytes=58 << 20),
        cost_estimate=pl.CostEstimate(flops=0, bytes_accessed=0, transcendentals=0),
        name="last_product" if final else "early_product",
    )(where, *pieces, *chunks, *([carried] if final else []))


def ring_order(count):
    return list(range(0, count, 2)) + list(range(count - 1, 0, -2))


def nothing(*refs):
    del refs


def fence(*values):
    hbm = pl.BlockSpec(memory_space=pl.ANY)
    return pl.pallas_call(
        nothing,
        out_shape=[jax.ShapeDtypeStruct(value.shape, value.dtype) for value in values],
        in_specs=[hbm] * len(values),
        out_specs=[hbm] * len(values),
        input_output_aliases={i: i for i in range(len(values))},
        name="fence",
    )(*values)


def shifted(value, pairs):
    return lax.ppermute(value, "vocab", pairs)


def merge_stats(stats, axis):
    count = lax.axis_size(axis)
    index = lax.axis_index(axis)
    mask = 1
    while mask < count:
        other = lax.ppermute(stats, axis, xor_perm(count, mask))
        upper = (index & mask) != 0
        first = jnp.where(upper, other, stats)
        second = jnp.where(upper, stats, other)
        peak = jnp.maximum(first[0], second[0])
        total = first[1] * jnp.exp(first[0] - peak) + second[1] * jnp.exp(second[0] - peak)
        stats = jnp.stack([peak, total, first[2] + second[2]])
        mask *= 2
    return stats


def body(src_embed, src_head, block_ids, slot_counts, slot_weights, hidden, targets, byte_counts):
    block_rows = slot_weights.shape[2]
    rows, quarter = src_embed.shape
    new_rows = slot_weights.shape[0] * block_rows
    vocab_index = lax.axis_index("vocab")
    halo = REACH * block_rows
    last_local = rows // block_rows + 2 * REACH - 1
    local_ids = jnp.clip(block_ids - (vocab_index * (rows // block_rows) - REACH), 0, last_local)

    count = lax.axis_size("vocab")
    tok_index, tok_count = lax.axis_index("tok"), lax.axis_size("tok")
    up = [(i, i + 1) for i in range(count - 1)]
    down = [(j, i) for i, j in up]
    bottom_edge, top_edge = src_embed[rows - halo :], src_embed[:halo]
    far = tok_count // 2
    near_masks = [1 << bit for bit in reversed(range(far.bit_length() - 1))]
    width = hidden.shape[1]

    def to_far(value):
        return lax.ppermute(value, "tok", xor_perm(tok_count, far))

    def spread(held_pieces):
        for mask in near_masks:
            for held in list(held_pieces):
                held_pieces[held | mask] = lax.ppermute(held_pieces[held], "tok", xor_perm(tok_count, mask))
        return held_pieces

    def assembled(held_pieces, start, size):
        whole = jnp.zeros((size, tok_count * quarter), src_head.dtype)
        for held, entries in held_pieces.items():
            for offset, entry in entries:
                whole = lax.dynamic_update_slice(whole, entry, (offset - start, (tok_index ^ held) * quarter))
        return whole

    def product(head, arrivals):
        total = None
        for origin, value in arrivals:
            columns = lax.dynamic_slice_in_dim(head, origin * width, value.shape[1], axis=1)
            part = lax.dot_general(columns, value, CONTRACT_LAST, preferred_element_type=jnp.float32)
            total = part if total is None else total + part
        return total

    if count == 8 and tok_count == 4:
        order = ring_order(count)
        at = jnp.where(vocab_index % 2 == 0, vocab_index // 2, count - 1 - vocab_index // 2)
        ahead = [(order[i], order[(i + 1) % count]) for i in range(count)]
        behind = [(j, i) for i, j in ahead]

        def origin(offset):
            place = (at + offset) % count
            return jnp.where(place < count // 2, 2 * place, 2 * (count - 1 - place) + 1)

        aside_pairs = [(2, 3), (3, 2), (4, 5), (5, 4)]
        up_pairs = [(0, 1), (1, 2), (2, 3), (3, 4), (4, 6), (6, 7)]
        down_pairs = [(1, 0), (3, 1), (4, 3), (5, 4), (6, 5), (7, 6)]
        side = jnp.where(vocab_index == 5, 1, jnp.where(vocab_index == 2, 2, 0))
        a1, b1 = lax.ppermute(hidden, "vocab", ahead), lax.ppermute(hidden, "vocab", behind)
        far_head = to_far(src_head)
        aside = shifted(jnp.where(vocab_index < 4, top_edge, bottom_edge), aside_pairs)
        near_head = spread({0: src_head})[1]
        a1, b1, aside, near_head = fence(a1, b1, aside, near_head)
        a2, b2 = lax.ppermute(a1, "vocab", ahead), lax.ppermute(b1, "vocab", behind)
        table_before = shifted(jnp.where(vocab_index == 4, aside, bottom_edge), up_pairs)
        table_after = shifted(jnp.where(vocab_index == 3, aside, top_edge), down_pairs)
        a2, b2, table_before, table_after = fence(a2, b2, table_before, table_after)
        a3, b3 = lax.ppermute(a2, "vocab", ahead), lax.ppermute(b2, "vocab", behind)
        new_embed = blend_table(
            local_ids, slot_counts, slot_weights, src_embed, table_before, table_after, aside, side.reshape(1)
        )
        a3, b3, new_embed, far_head = fence(a3, b3, new_embed, far_head)
        even = tok_index % 2 == 0
        last_pairs = [
            (i * tok_count + t, j * tok_count + t) for t in range(tok_count) for i, j in (behind if t % 2 else ahead)
        ]
        c4 = lax.ppermute(jnp.where(even, a3, b3), ("vocab", "tok"), last_pairs)
        far_near_head = spread({far: far_head})[far | 1]
        pieces = [src_head, near_head, far_head, far_near_head]
        per = count // tok_count
        where = lambda offsets: jnp.stack(
            [jnp.stack([(origin(o) // per) ^ tok_index for o in offsets]), jnp.stack([origin(o) % per for o in offsets])]
        ).astype(jnp.int32)
        (early,) = add_products(where([0, -1, 1, -2, 2, -3, 3]), pieces, [hidden, a1, b1, a2, b2, a3, b3])
        source_logits = add_products(where([4]), pieces, [c4], early, (halo, rows - 2 * halo, halo))
    else:
        pieces = spread({0: src_head, far: to_far(src_head)})
        whole_head = assembled({held: [(0, piece)] for held, piece in pieces.items()}, 0, rows)
        whole_rows = lax.all_gather(hidden, "vocab", axis=1, tiled=True)
        total = product(whole_head, [(0, whole_rows)]).astype(jnp.bfloat16)
        source_logits = [total[:halo], total[halo : rows - halo], total[rows - halo :]]
        table_before, table_after = shifted(bottom_edge, up), shifted(top_edge, down)
        new_embed = blend_table(
            local_ids, slot_counts, slot_weights, src_embed, table_before, table_after, table_before, jnp.zeros((1,), jnp.int32)
        )
    after_rows = shifted(source_logits[0], down)
    before_rows = shifted(source_logits[-1], up)
    goals = (targets - vocab_index * new_rows)[None, :]
    stats = local_stats(local_ids, slot_counts, slot_weights, [before_rows] + list(source_logits) + [after_rows], goals)
    stats = merge_stats(stats, "vocab")
    log_total = stats[0] + jnp.log(stats[1])
    token_bpb = (log_total - stats[2]) / (jnp.float32(math.log(2.0)) * byte_counts.astype(jnp.float32))

    return (new_embed, token_bpb)


def solution(mesh):
    in_specs = (
        P("vocab", "tok"),
        P("vocab", "tok"),
        P("vocab", None),
        P("vocab"),
        P("vocab", None, None, None),
        P("tok", "vocab"),
        P("tok"),
        P("tok"),
    )
    out_specs = (P("vocab", "tok"), P("tok"))
    return jax.shard_map(body, mesh=mesh, in_specs=in_specs, out_specs=out_specs, check_vma=False)
```

```python
import functools
import math

import jax
import jax.numpy as jnp
from jax import lax
from jax.experimental import pallas as pl
from jax.experimental.pallas import tpu as pltpu
from jax.sharding import PartitionSpec as P

REACH = 2
CONTRACT_LAST = (((1,), (1,)), ((), ()))


def xor_perm(count, mask):
    return [(i, i ^ mask) for i in range(count)]


def masked(weights, slot, amount):
    return jnp.where(slot < amount, weights, jnp.zeros_like(weights))


def blend_block(ids_ref, counts_ref, weights_ref, padded, block):
    slots, rows = weights_ref.shape[1], weights_ref.shape[2]
    total = None
    for slot in range(slots):
        start = pl.multiple_of(ids_ref[block, slot] * rows, rows)
        part = jnp.dot(
            masked(weights_ref[block, slot], slot, counts_ref[block]),
            padded[pl.ds(start, rows), :],
            preferred_element_type=jnp.float32,
        )
        total = part if total is None else total + part
    return total


def table_kernel(ids_ref, counts_ref, side_ref, weights_ref, own_ref, before_ref, after_ref, relayed_ref, out_ref, padded):
    edge, own_rows = before_ref.shape[0], own_ref.shape[0]
    padded[pl.ds(0, edge), :] = before_ref[...]
    padded[pl.ds(edge, own_rows), :] = own_ref[...]
    padded[pl.ds(edge + own_rows, edge), :] = after_ref[...]

    @pl.when(side_ref[0] == 1)
    def _():
        padded[pl.ds(0, edge), :] = relayed_ref[...]

    @pl.when(side_ref[0] == 2)
    def _():
        padded[pl.ds(edge + own_rows, edge), :] = relayed_ref[...]

    blocks, rows = weights_ref.shape[0], weights_ref.shape[2]
    for block in range(blocks):
        summed = blend_block(ids_ref, counts_ref, weights_ref, padded, block)
        out_ref[pl.ds(block * rows, rows), :] = summed.astype(out_ref.dtype)


def blend_table(ids, counts, weights, own, before, after, relayed, side, tile=512):
    rows, columns = own.shape
    edge = before.shape[0]
    tile = math.gcd(tile, columns)
    smem = pl.BlockSpec(memory_space=pltpu.SMEM)
    strip = lambda count: pl.BlockSpec((count, tile), lambda i: (0, i))
    new_rows = weights.shape[0] * weights.shape[2]
    return pl.pallas_call(
        table_kernel,
        grid=(columns // tile,),
        out_shape=jax.ShapeDtypeStruct((new_rows, columns), own.dtype),
        in_specs=[smem, smem, smem, pl.BlockSpec(weights.shape, lambda i: (0, 0, 0, 0)), strip(rows)] + [strip(edge)] * 3,
        out_specs=strip(new_rows),
        scratch_shapes=[pltpu.VMEM((rows + 2 * edge, tile), own.dtype)],
        compiler_params=pltpu.CompilerParams(vmem_limit_bytes=32 << 20),
        cost_estimate=pl.CostEstimate(
            flops=0, bytes_accessed=0, transcendentals=0
        ),
        name="blend_table",
    )(ids, counts, side, weights, own, before, after, relayed)


def stats_kernel(ids_ref, counts_ref, weights_ref, *refs):
    *source_refs, goals_ref, out_ref, padded, logits = refs
    start = 0
    for source_ref in source_refs:
        padded[pl.ds(start, source_ref.shape[0]), :] = source_ref[...]
        start += source_ref.shape[0]
    blocks, rows = weights_ref.shape[0], weights_ref.shape[2]
    tokens = padded.shape[1]
    goals = goals_ref[...]
    peak = jnp.full((1, tokens), -jnp.inf, jnp.float32)
    picked = jnp.zeros((1, tokens), jnp.float32)
    for block in range(blocks):
        summed = blend_block(ids_ref, counts_ref, weights_ref, padded, block)
        logits[pl.ds(block * rows, rows), :] = summed
        peak = jnp.maximum(peak, jnp.max(summed, axis=0, keepdims=True))
        row_ids = lax.broadcasted_iota(jnp.int32, summed.shape, 0) + block * rows
        picked = picked + jnp.sum(jnp.where(row_ids == goals, summed, 0.0), axis=0, keepdims=True)
    total = jnp.zeros((1, tokens), jnp.float32)
    for block in range(blocks):
        values = jnp.exp(logits[pl.ds(block * rows, rows), :] - peak)
        total = total + jnp.sum(values, axis=0, keepdims=True)
    out_ref[0:1, :] = peak
    out_ref[1:2, :] = total
    out_ref[2:3, :] = picked


def local_stats(ids, counts, weights, source, goals):
    tokens = source[0].shape[1]
    source_rows = sum(value.shape[0] for value in source)
    smem = pl.BlockSpec(memory_space=pltpu.SMEM)
    vmem = pl.BlockSpec(memory_space=pltpu.VMEM)
    new_rows = weights.shape[0] * weights.shape[2]
    return pl.pallas_call(
        stats_kernel,
        out_shape=jax.ShapeDtypeStruct((3, tokens), jnp.float32),
        in_specs=[smem, smem, vmem] + [vmem] * (len(source) + 1),
        out_specs=vmem,
        scratch_shapes=[
            pltpu.VMEM((source_rows, tokens), source[0].dtype),
            pltpu.VMEM((new_rows, tokens), jnp.float32),
        ],
        compiler_params=pltpu.CompilerParams(vmem_limit_bytes=32 << 20),
        cost_estimate=pl.CostEstimate(
            flops=2 * weights.size * tokens, bytes_accessed=2 * source_rows * tokens, transcendentals=new_rows * tokens
        ),
        name="blend_stats",
    )(ids, counts, weights, *source, goals)


def product_kernel(where_ref, *refs, pieces, chunks, bands, skipped, only, final):
    piece_refs, refs = refs[:pieces], refs[pieces:]
    chunk_refs, refs = refs[:chunks], refs[chunks:]
    carried_ref, refs = (refs[0], refs[1:]) if final else (None, refs)
    out_refs, (total, held, block, sems) = refs[:-4], refs[-4:]
    width = held.shape[2]

    def copies(at, piece_ref):
        start = pl.multiple_of(where_ref[1, at] * width, width)
        row = 0
        for band, (first, size) in enumerate(bands):
            yield pltpu.make_async_copy(
                piece_ref.at[pl.ds(first, size), pl.ds(start, width)],
                held.at[at, pl.ds(row, size), :],
                sems.at[1 + band, at],
            )
            row += size

    def block_copy(at):
        return pltpu.make_async_copy(chunk_refs[at], block.at[at], sems.at[0, at])

    def wanted(at):
        if only and at == chunks - 1:
            return where_ref[0, at] >= 0
        return (where_ref[0, at] == skipped) if only else (where_ref[0, at] != skipped)

    for at in range(chunks):
        @pl.when(wanted(at))
        def _(at=at):
            block_copy(at).start()

        for piece, piece_ref in enumerate(piece_refs):
            @pl.when(wanted(at) & (where_ref[0, at] == piece))
            def _(at=at, piece_ref=piece_ref):
                for copy in copies(at, piece_ref):
                    copy.start()

    if final:
        row = 0
        for first, size in bands:
            total[pl.ds(row, size), :] = carried_ref[pl.ds(first, size), :]
            row += size
    else:
        total[...] = jnp.zeros_like(total)
    for at in range(chunks):
        @pl.when(wanted(at))
        def _(at=at):
            block_copy(at).wait()
            for copy in copies(at, piece_refs[0]):
                copy.wait()
            total[...] += lax.dot_general(held[at], block[at], CONTRACT_LAST, preferred_element_type=jnp.float32)

    row = 0
    for out_ref in out_refs:
        out_ref[...] = total[pl.ds(row, out_ref.shape[0]), :].astype(out_ref.dtype)
        row += out_ref.shape[0]


def add_products(where, pieces, chunks, bands, skipped, carried=None):
    tokens, width = chunks[0].shape
    rows = sum(size for _, size in bands)
    final = carried is not None
    vmem = pl.BlockSpec(memory_space=pltpu.VMEM)
    hbm = pl.BlockSpec(memory_space=pltpu.HBM)
    if final:
        shapes = [jax.ShapeDtypeStruct((size, tokens), jnp.bfloat16) for _, size in bands]
    else:
        shapes = [jax.ShapeDtypeStruct((rows, tokens), jnp.float32)]
    return pl.pallas_call(
        functools.partial(
            product_kernel, pieces=len(pieces), chunks=len(chunks), bands=bands, skipped=skipped, only=final, final=final
        ),
        out_shape=shapes,
        in_specs=[pl.BlockSpec(memory_space=pltpu.SMEM)] + [hbm] * (len(pieces) + len(chunks)) + [vmem] * final,
        out_specs=[vmem] * len(shapes),
        scratch_shapes=[
            pltpu.VMEM((rows, tokens), jnp.float32),
            pltpu.VMEM((len(chunks), rows, width), jnp.bfloat16),
            pltpu.VMEM((len(chunks), tokens, width), jnp.bfloat16),
            pltpu.SemaphoreType.DMA((1 + len(bands), len(chunks))),
        ],
        compiler_params=pltpu.CompilerParams(vmem_limit_bytes=(52 if final else 58) << 20),
        cost_estimate=pl.CostEstimate(flops=0, bytes_accessed=0, transcendentals=0),
        name="last_product" if final else "early_product",
    )(where, *pieces, *chunks, *([carried] if final else []))


def ring_order(count):
    return list(range(0, count, 2)) + list(range(count - 1, 0, -2))


def nothing(*refs):
    del refs


def fence(*values):
    hbm = pl.BlockSpec(memory_space=pl.ANY)
    return pl.pallas_call(
        nothing,
        out_shape=[jax.ShapeDtypeStruct(value.shape, value.dtype) for value in values],
        in_specs=[hbm] * len(values),
        out_specs=[hbm] * len(values),
        input_output_aliases={i: i for i in range(len(values))},
        name="fence",
    )(*values)


def shifted(value, pairs):
    return lax.ppermute(value, "vocab", pairs)


def merge_stats(stats, axis):
    count = lax.axis_size(axis)
    index = lax.axis_index(axis)
    mask = 1
    while mask < count:
        other = lax.ppermute(stats, axis, xor_perm(count, mask))
        upper = (index & mask) != 0
        first = jnp.where(upper, other, stats)
        second = jnp.where(upper, stats, other)
        peak = jnp.maximum(first[0], second[0])
        total = first[1] * jnp.exp(first[0] - peak) + second[1] * jnp.exp(second[0] - peak)
        stats = jnp.stack([peak, total, first[2] + second[2]])
        mask *= 2
    return stats


def body(src_embed, src_head, block_ids, slot_counts, slot_weights, hidden, targets, byte_counts):
    block_rows = slot_weights.shape[2]
    rows, quarter = src_embed.shape
    new_rows = slot_weights.shape[0] * block_rows
    vocab_index = lax.axis_index("vocab")
    halo = REACH * block_rows
    last_local = rows // block_rows + 2 * REACH - 1
    local_ids = jnp.clip(block_ids - (vocab_index * (rows // block_rows) - REACH), 0, last_local)

    count = lax.axis_size("vocab")
    tok_index, tok_count = lax.axis_index("tok"), lax.axis_size("tok")
    up = [(i, i + 1) for i in range(count - 1)]
    down = [(j, i) for i, j in up]
    bottom_edge, top_edge = src_embed[rows - halo :], src_embed[:halo]
    far = tok_count // 2
    near_masks = [1 << bit for bit in reversed(range(far.bit_length() - 1))]
    width = hidden.shape[1]

    def to_far(value):
        return lax.ppermute(value, "tok", xor_perm(tok_count, far))

    def spread(held_pieces):
        for mask in near_masks:
            for held in list(held_pieces):
                held_pieces[held | mask] = lax.ppermute(held_pieces[held], "tok", xor_perm(tok_count, mask))
        return held_pieces

    def assembled(held_pieces, start, size):
        whole = jnp.zeros((size, tok_count * quarter), src_head.dtype)
        for held, entries in held_pieces.items():
            for offset, entry in entries:
                whole = lax.dynamic_update_slice(whole, entry, (offset - start, (tok_index ^ held) * quarter))
        return whole

    def product(head, arrivals):
        total = None
        for origin, value in arrivals:
            columns = lax.dynamic_slice_in_dim(head, origin * width, value.shape[1], axis=1)
            part = lax.dot_general(columns, value, CONTRACT_LAST, preferred_element_type=jnp.float32)
            total = part if total is None else total + part
        return total

    if count == 8 and tok_count == 4:
        order = ring_order(count)
        at = jnp.where(vocab_index % 2 == 0, vocab_index // 2, count - 1 - vocab_index // 2)
        ahead = [(order[i], order[(i + 1) % count]) for i in range(count)]
        behind = [(j, i) for i, j in ahead]

        def origin(offset):
            place = (at + offset) % count
            return jnp.where(place < count // 2, 2 * place, 2 * (count - 1 - place) + 1)

        aside_pairs = [(2, 3), (3, 2), (4, 5), (5, 4)]
        up_pairs = [(0, 1), (1, 2), (2, 3), (3, 4), (4, 6), (6, 7)]
        down_pairs = [(1, 0), (3, 1), (4, 3), (5, 4), (6, 5), (7, 6)]
        side = jnp.where(vocab_index == 5, 1, jnp.where(vocab_index == 2, 2, 0))
        a1, b1 = lax.ppermute(hidden, "vocab", ahead), lax.ppermute(hidden, "vocab", behind)
        far_head = to_far(src_head)
        aside = shifted(jnp.where(vocab_index < 4, top_edge, bottom_edge), aside_pairs)
        near_head = spread({0: src_head})[1]
        a1, b1, near_head = fence(a1, b1, near_head)
        a2, b2 = lax.ppermute(a1, "vocab", ahead), lax.ppermute(b1, "vocab", behind)
        table_before = shifted(jnp.where(vocab_index == 4, aside, bottom_edge), up_pairs)
        table_after = shifted(jnp.where(vocab_index == 3, aside, top_edge), down_pairs)
        a2, b2 = fence(a2, b2)
        a3, b3 = lax.ppermute(a2, "vocab", ahead), lax.ppermute(b2, "vocab", behind)
        new_embed = blend_table(
            local_ids, slot_counts, slot_weights, src_embed, table_before, table_after, aside, side.reshape(1)
        )
        a3, b3, new_embed, far_head = fence(a3, b3, new_embed, far_head)
        even = tok_index % 2 == 0
        last_pairs = [
            (i * tok_count + t, j * tok_count + t) for t in range(tok_count) for i, j in (behind if t % 2 else ahead)
        ]
        c4 = lax.ppermute(jnp.where(even, a3, b3), ("vocab", "tok"), last_pairs)
        far_near_head = spread({far: far_head})[far | 1]
        pieces = [src_head, near_head, far_head, far_near_head]
        per = count // tok_count
        where = lambda offsets: jnp.stack(
            [jnp.stack([(origin(o) // per) ^ tok_index for o in offsets]), jnp.stack([origin(o) % per for o in offsets])]
        ).astype(jnp.int32)
        early_offsets = [0, -1, 1, -2, 2, -3, 3]
        blocks = [hidden, a1, b1, a2, b2, a3, b3]
        (early,) = add_products(where(early_offsets), pieces[:3], blocks, [(0, rows)], 3)
        late = lambda bands: add_products(where(early_offsets + [4]), pieces, blocks + [c4], bands, 3, early)
        top_logits, bottom_logits = late([(0, halo), (rows - halo, halo)])
        (middle_logits,) = late([(halo, rows - 2 * halo)])
        source_logits = [top_logits, middle_logits, bottom_logits]
    else:
        pieces = spread({0: src_head, far: to_far(src_head)})
        whole_head = assembled({held: [(0, piece)] for held, piece in pieces.items()}, 0, rows)
        whole_rows = lax.all_gather(hidden, "vocab", axis=1, tiled=True)
        total = product(whole_head, [(0, whole_rows)]).astype(jnp.bfloat16)
        source_logits = [total[:halo], total[halo : rows - halo], total[rows - halo :]]
        table_before, table_after = shifted(bottom_edge, up), shifted(top_edge, down)
        new_embed = blend_table(
            local_ids, slot_counts, slot_weights, src_embed, table_before, table_after, table_before, jnp.zeros((1,), jnp.int32)
        )
    after_rows = shifted(source_logits[0], down)
    before_rows = shifted(source_logits[-1], up)
    goals = (targets - vocab_index * new_rows)[None, :]
    stats = local_stats(local_ids, slot_counts, slot_weights, [before_rows] + list(source_logits) + [after_rows], goals)
    stats = merge_stats(stats, "vocab")
    log_total = stats[0] + jnp.log(stats[1])
    token_bpb = (log_total - stats[2]) / (jnp.float32(math.log(2.0)) * byte_counts.astype(jnp.float32))

    return (new_embed, token_bpb)


def solution(mesh):
    in_specs = (
        P("vocab", "tok"),
        P("vocab", "tok"),
        P("vocab", None),
        P("vocab"),
        P("vocab", None, None, None),
        P("tok", "vocab"),
        P("tok"),
        P("tok"),
    )
    out_specs = (P("vocab", "tok"), P("tok"))
    return jax.shard_map(body, mesh=mesh, in_specs=in_specs, out_specs=out_specs, check_vma=False)
```

```python
import functools
import math

import jax
import jax.numpy as jnp
from jax import lax
from jax.experimental import pallas as pl
from jax.experimental.pallas import tpu as pltpu
from jax.sharding import PartitionSpec as P

REACH = 2
CONTRACT_LAST = (((1,), (1,)), ((), ()))


def xor_perm(count, mask):
    return [(i, i ^ mask) for i in range(count)]


def masked(weights, slot, amount):
    return jnp.where(slot < amount, weights, jnp.zeros_like(weights))


def blend_block(ids_ref, counts_ref, weights_ref, padded, block):
    slots, rows = weights_ref.shape[1], weights_ref.shape[2]
    total = None
    for slot in range(slots):
        start = pl.multiple_of(ids_ref[block, slot] * rows, rows)
        part = jnp.dot(
            masked(weights_ref[block, slot], slot, counts_ref[block]),
            padded[pl.ds(start, rows), :],
            preferred_element_type=jnp.float32,
        )
        total = part if total is None else total + part
    return total


def table_kernel(ids_ref, counts_ref, side_ref, weights_ref, own_ref, before_ref, after_ref, relayed_ref, out_ref, padded):
    edge, own_rows = before_ref.shape[0], own_ref.shape[0]
    padded[pl.ds(0, edge), :] = before_ref[...]
    padded[pl.ds(edge, own_rows), :] = own_ref[...]
    padded[pl.ds(edge + own_rows, edge), :] = after_ref[...]

    @pl.when(side_ref[0] == 1)
    def _():
        padded[pl.ds(0, edge), :] = relayed_ref[...]

    @pl.when(side_ref[0] == 2)
    def _():
        padded[pl.ds(edge + own_rows, edge), :] = relayed_ref[...]

    blocks, rows = weights_ref.shape[0], weights_ref.shape[2]
    for block in range(blocks):
        summed = blend_block(ids_ref, counts_ref, weights_ref, padded, block)
        out_ref[pl.ds(block * rows, rows), :] = summed.astype(out_ref.dtype)


def blend_table(ids, counts, weights, own, before, after, relayed, side, tile=512):
    rows, columns = own.shape
    edge = before.shape[0]
    tile = math.gcd(tile, columns)
    smem = pl.BlockSpec(memory_space=pltpu.SMEM)
    strip = lambda count: pl.BlockSpec((count, tile), lambda i: (0, i))
    new_rows = weights.shape[0] * weights.shape[2]
    return pl.pallas_call(
        table_kernel,
        grid=(columns // tile,),
        out_shape=jax.ShapeDtypeStruct((new_rows, columns), own.dtype),
        in_specs=[smem, smem, smem, pl.BlockSpec(weights.shape, lambda i: (0, 0, 0, 0)), strip(rows)] + [strip(edge)] * 3,
        out_specs=strip(new_rows),
        scratch_shapes=[pltpu.VMEM((rows + 2 * edge, tile), own.dtype)],
        compiler_params=pltpu.CompilerParams(vmem_limit_bytes=32 << 20),
        cost_estimate=pl.CostEstimate(
            flops=0, bytes_accessed=0, transcendentals=0
        ),
        name="blend_table",
    )(ids, counts, side, weights, own, before, after, relayed)


def stats_kernel(ids_ref, counts_ref, weights_ref, *refs):
    *source_refs, goals_ref, out_ref, padded, logits = refs
    start = 0
    for source_ref in source_refs:
        padded[pl.ds(start, source_ref.shape[0]), :] = source_ref[...]
        start += source_ref.shape[0]
    blocks, rows = weights_ref.shape[0], weights_ref.shape[2]
    tokens = padded.shape[1]
    goals = goals_ref[...]
    peak = jnp.full((1, tokens), -jnp.inf, jnp.float32)
    picked = jnp.zeros((1, tokens), jnp.float32)
    for block in range(blocks):
        summed = blend_block(ids_ref, counts_ref, weights_ref, padded, block)
        logits[pl.ds(block * rows, rows), :] = summed
        peak = jnp.maximum(peak, jnp.max(summed, axis=0, keepdims=True))
        row_ids = lax.broadcasted_iota(jnp.int32, summed.shape, 0) + block * rows
        picked = picked + jnp.sum(jnp.where(row_ids == goals, summed, 0.0), axis=0, keepdims=True)
    total = jnp.zeros((1, tokens), jnp.float32)
    for block in range(blocks):
        values = jnp.exp(logits[pl.ds(block * rows, rows), :] - peak)
        total = total + jnp.sum(values, axis=0, keepdims=True)
    out_ref[0:1, :] = peak
    out_ref[1:2, :] = total
    out_ref[2:3, :] = picked


def local_stats(ids, counts, weights, source, goals):
    tokens = source[0].shape[1]
    source_rows = sum(value.shape[0] for value in source)
    smem = pl.BlockSpec(memory_space=pltpu.SMEM)
    vmem = pl.BlockSpec(memory_space=pltpu.VMEM)
    new_rows = weights.shape[0] * weights.shape[2]
    return pl.pallas_call(
        stats_kernel,
        out_shape=jax.ShapeDtypeStruct((3, tokens), jnp.float32),
        in_specs=[smem, smem, vmem] + [vmem] * (len(source) + 1),
        out_specs=vmem,
        scratch_shapes=[
            pltpu.VMEM((source_rows, tokens), source[0].dtype),
            pltpu.VMEM((new_rows, tokens), jnp.float32),
        ],
        compiler_params=pltpu.CompilerParams(vmem_limit_bytes=32 << 20),
        cost_estimate=pl.CostEstimate(
            flops=2 * weights.size * tokens, bytes_accessed=2 * source_rows * tokens, transcendentals=new_rows * tokens
        ),
        name="blend_stats",
    )(ids, counts, weights, *source, goals)


def product_kernel(where_ref, *refs, pieces, chunks, bands, final):
    piece_refs, refs = refs[:pieces], refs[pieces:]
    chunk_refs, refs = refs[:chunks], refs[chunks:]
    carried_ref, refs = (refs[0], refs[1:]) if final else (None, refs)
    out_refs, (total, held, block, sems) = refs[:-4], refs[-4:]
    width = held.shape[2]
    rows_at = [sum(size for _, size in bands[:band]) for band in range(len(bands))]

    def copies(at, piece_ref):
        start = pl.multiple_of(where_ref[1, at] * width, width)
        for band, (first, size) in enumerate(bands):
            yield pltpu.make_async_copy(
                piece_ref.at[pl.ds(first, size), pl.ds(start, width)],
                held.at[at, pl.ds(rows_at[band], size), :],
                sems.at[1 + band, at],
            )

    def block_copy(at):
        return pltpu.make_async_copy(chunk_refs[at], block.at[at], sems.at[0, at])

    def carried_copies():
        for band, (first, size) in enumerate(bands):
            yield pltpu.make_async_copy(
                carried_ref.at[pl.ds(first, size), :], total.at[pl.ds(rows_at[band], size), :], sems.at[1 + band, chunks]
            )

    if final:
        for copy in carried_copies():
            copy.start()
    else:
        total[...] = jnp.zeros_like(total)
    for at in range(chunks):
        @pl.when(where_ref[2, at] == 1)
        def _(at=at):
            block_copy(at).start()

        for piece, piece_ref in enumerate(piece_refs):
            @pl.when((where_ref[2, at] == 1) & (where_ref[0, at] == piece))
            def _(at=at, piece_ref=piece_ref):
                for copy in copies(at, piece_ref):
                    copy.start()

    if final:
        for copy in carried_copies():
            copy.wait()
    for at in range(chunks):
        @pl.when(where_ref[2, at] == 1)
        def _(at=at):
            block_copy(at).wait()
            for copy in copies(at, piece_refs[0]):
                copy.wait()
            total[...] += lax.dot_general(held[at], block[at], CONTRACT_LAST, preferred_element_type=jnp.float32)

    for out_ref, row in zip(out_refs, rows_at):
        out_ref[...] = total[pl.ds(row, out_ref.shape[0]), :].astype(out_ref.dtype)


def add_products(where, pieces, chunks, bands, carried=None):
    tokens, width = chunks[0].shape
    rows = sum(size for _, size in bands)
    final = carried is not None
    vmem = pl.BlockSpec(memory_space=pltpu.VMEM)
    hbm = pl.BlockSpec(memory_space=pltpu.HBM)
    if final:
        shapes = [jax.ShapeDtypeStruct((size, tokens), jnp.bfloat16) for _, size in bands]
    else:
        shapes = [jax.ShapeDtypeStruct((rows, tokens), jnp.float32)]
    return pl.pallas_call(
        functools.partial(product_kernel, pieces=len(pieces), chunks=len(chunks), bands=bands, final=final),
        out_shape=shapes,
        in_specs=[pl.BlockSpec(memory_space=pltpu.SMEM)] + [hbm] * (len(pieces) + len(chunks) + final),
        out_specs=[vmem] * len(shapes),
        scratch_shapes=[
            pltpu.VMEM((rows, tokens), jnp.float32),
            pltpu.VMEM((len(chunks), rows, width), jnp.bfloat16),
            pltpu.VMEM((len(chunks), tokens, width), jnp.bfloat16),
            pltpu.SemaphoreType.DMA((1 + len(bands), len(chunks) + 1)),
        ],
        compiler_params=pltpu.CompilerParams(vmem_limit_bytes=(52 if final else 58) << 20),
        cost_estimate=pl.CostEstimate(flops=0, bytes_accessed=0, transcendentals=0),
        name="last_product" if final else "early_product",
    )(where, *pieces, *chunks, *([carried] if final else []))


def ring_order(count):
    return list(range(0, count, 2)) + list(range(count - 1, 0, -2))


def nothing(*refs):
    del refs


def fence(*values):
    hbm = pl.BlockSpec(memory_space=pl.ANY)
    return pl.pallas_call(
        nothing,
        out_shape=[jax.ShapeDtypeStruct(value.shape, value.dtype) for value in values],
        in_specs=[hbm] * len(values),
        out_specs=[hbm] * len(values),
        input_output_aliases={i: i for i in range(len(values))},
        name="fence",
    )(*values)


def shifted(value, pairs):
    return lax.ppermute(value, "vocab", pairs)


def merge_stats(stats, axis):
    count = lax.axis_size(axis)
    index = lax.axis_index(axis)
    low = 1
    while low < count:
        group = min(4, count // low)
        place = (index // low) % group
        got = [stats] + [lax.ppermute(stats, axis, xor_perm(count, low * mask)) for mask in range(1, group)]
        ordered = []
        for at in range(group):
            value = got[0]
            for mask in range(1, group):
                value = jnp.where((place ^ mask) == at, got[mask], value)
            ordered.append(value)
        peak = functools.reduce(jnp.maximum, [value[0] for value in ordered])
        total = sum(value[1] * jnp.exp(value[0] - peak) for value in ordered)
        stats = jnp.stack([peak, total, sum(value[2] for value in ordered)])
        low *= group
    return stats


def body(src_embed, src_head, block_ids, slot_counts, slot_weights, hidden, targets, byte_counts):
    block_rows = slot_weights.shape[2]
    rows, quarter = src_embed.shape
    new_rows = slot_weights.shape[0] * block_rows
    vocab_index = lax.axis_index("vocab")
    halo = REACH * block_rows
    last_local = rows // block_rows + 2 * REACH - 1
    local_ids = jnp.clip(block_ids - (vocab_index * (rows // block_rows) - REACH), 0, last_local)

    count = lax.axis_size("vocab")
    tok_index, tok_count = lax.axis_index("tok"), lax.axis_size("tok")
    up = [(i, i + 1) for i in range(count - 1)]
    down = [(j, i) for i, j in up]
    bottom_edge, top_edge = src_embed[rows - halo :], src_embed[:halo]
    far = tok_count // 2
    near_masks = [1 << bit for bit in reversed(range(far.bit_length() - 1))]
    width = hidden.shape[1]

    def to_far(value):
        return lax.ppermute(value, "tok", xor_perm(tok_count, far))

    def spread(held_pieces):
        for mask in near_masks:
            for held in list(held_pieces):
                held_pieces[held | mask] = lax.ppermute(held_pieces[held], "tok", xor_perm(tok_count, mask))
        return held_pieces

    def assembled(held_pieces, start, size):
        whole = jnp.zeros((size, tok_count * quarter), src_head.dtype)
        for held, entries in held_pieces.items():
            for offset, entry in entries:
                whole = lax.dynamic_update_slice(whole, entry, (offset - start, (tok_index ^ held) * quarter))
        return whole

    def product(head, arrivals):
        total = None
        for origin, value in arrivals:
            columns = lax.dynamic_slice_in_dim(head, origin * width, value.shape[1], axis=1)
            part = lax.dot_general(columns, value, CONTRACT_LAST, preferred_element_type=jnp.float32)
            total = part if total is None else total + part
        return total

    if count == 8 and tok_count == 4:
        order = ring_order(count)
        at = jnp.where(vocab_index % 2 == 0, vocab_index // 2, count - 1 - vocab_index // 2)
        ahead = [(order[i], order[(i + 1) % count]) for i in range(count)]
        behind = [(j, i) for i, j in ahead]

        def origin(offset):
            place = (at + offset) % count
            return jnp.where(place < count // 2, 2 * place, 2 * (count - 1 - place) + 1)

        aside_pairs = [(2, 3), (3, 2), (4, 5), (5, 4)]
        up_pairs = [(0, 1), (1, 2), (2, 3), (3, 4), (4, 6), (6, 7)]
        down_pairs = [(1, 0), (3, 1), (4, 3), (5, 4), (6, 5), (7, 6)]
        side = jnp.where(vocab_index == 5, 1, jnp.where(vocab_index == 2, 2, 0))
        a1, b1 = lax.ppermute(hidden, "vocab", ahead), lax.ppermute(hidden, "vocab", behind)
        far_head = to_far(src_head)
        aside = shifted(jnp.where(vocab_index < 4, top_edge, bottom_edge), aside_pairs)
        near_head = spread({0: src_head})[1]
        a1, b1, near_head = fence(a1, b1, near_head)
        a2, b2 = lax.ppermute(a1, "vocab", ahead), lax.ppermute(b1, "vocab", behind)
        table_before = shifted(jnp.where(vocab_index == 4, aside, bottom_edge), up_pairs)
        table_after = shifted(jnp.where(vocab_index == 3, aside, top_edge), down_pairs)
        a2, b2 = fence(a2, b2)
        a3, b3 = lax.ppermute(a2, "vocab", ahead), lax.ppermute(b2, "vocab", behind)
        new_embed = blend_table(
            local_ids, slot_counts, slot_weights, src_embed, table_before, table_after, aside, side.reshape(1)
        )
        a3, b3, new_embed, far_head = fence(a3, b3, new_embed, far_head)
        def some(pairs, parity):
            return [(i * tok_count + t, j * tok_count + t) for t in range(parity, tok_count, 2) for i, j in pairs]

        even = (tok_index % 2 == 0).astype(jnp.int32)
        a4 = lax.ppermute(a3, ("vocab", "tok"), some(ahead, 0))
        b4 = lax.ppermute(b3, ("vocab", "tok"), some(behind, 1))
        far_near_head = spread({far: far_head})[far | 1]
        pieces = [src_head, near_head, far_head, far_near_head]
        per = count // tok_count
        offsets = [0, -1, 1, -2, 2, -3, 3, 4, 4]
        origins = jnp.stack([origin(offset) for offset in offsets]).astype(jnp.int32)
        piece_of = (origins // per) ^ tok_index
        late_piece = (piece_of == 3).astype(jnp.int32)
        wanted = jnp.concatenate([late_piece[:7], jnp.stack([even, 1 - even])])
        early_where = jnp.stack([piece_of, origins % per, 1 - late_piece])[:, :7]
        late_where = jnp.stack([piece_of, origins % per, wanted])
        blocks = [hidden, a1, b1, a2, b2, a3, b3]
        (early,) = add_products(early_where, pieces[:3], blocks, [(0, rows)])
        late = lambda bands: add_products(late_where, pieces, blocks + [a4, b4], bands, early)
        top_logits, bottom_logits = late([(0, halo), (rows - halo, halo)])
        (middle_logits,) = late([(halo, rows - 2 * halo)])
        source_logits = [top_logits, middle_logits, bottom_logits]
    else:
        pieces = spread({0: src_head, far: to_far(src_head)})
        whole_head = assembled({held: [(0, piece)] for held, piece in pieces.items()}, 0, rows)
        whole_rows = lax.all_gather(hidden, "vocab", axis=1, tiled=True)
        total = product(whole_head, [(0, whole_rows)]).astype(jnp.bfloat16)
        source_logits = [total[:halo], total[halo : rows - halo], total[rows - halo :]]
        table_before, table_after = shifted(bottom_edge, up), shifted(top_edge, down)
        new_embed = blend_table(
            local_ids, slot_counts, slot_weights, src_embed, table_before, table_after, table_before, jnp.zeros((1,), jnp.int32)
        )
    after_rows = shifted(source_logits[0], down)
    before_rows = shifted(source_logits[-1], up)
    goals = (targets - vocab_index * new_rows)[None, :]
    stats = local_stats(local_ids, slot_counts, slot_weights, [before_rows] + list(source_logits) + [after_rows], goals)
    stats = merge_stats(stats, "vocab")
    log_total = stats[0] + jnp.log(stats[1])
    token_bpb = (log_total - stats[2]) / (jnp.float32(math.log(2.0)) * byte_counts.astype(jnp.float32))

    return (new_embed, token_bpb)


def solution(mesh):
    in_specs = (
        P("vocab", "tok"),
        P("vocab", "tok"),
        P("vocab", None),
        P("vocab"),
        P("vocab", None, None, None),
        P("tok", "vocab"),
        P("tok"),
        P("tok"),
    )
    out_specs = (P("vocab", "tok"), P("tok"))
    return jax.shard_map(body, mesh=mesh, in_specs=in_specs, out_specs=out_specs, check_vma=False)
```

```python
import functools
import math

import jax
import jax.numpy as jnp
from jax import lax
from jax.experimental import pallas as pl
from jax.experimental.pallas import tpu as pltpu
from jax.sharding import PartitionSpec as P

REACH = 2
CONTRACT_LAST = (((1,), (1,)), ((), ()))


def xor_perm(count, mask):
    return [(i, i ^ mask) for i in range(count)]


def masked(weights, slot, amount):
    return jnp.where(slot < amount, weights, jnp.zeros_like(weights))


def blend_block(ids_ref, counts_ref, weights_ref, padded, block):
    slots, rows = weights_ref.shape[1], weights_ref.shape[2]
    total = None
    for slot in range(slots):
        start = pl.multiple_of(ids_ref[block, slot] * rows, rows)
        part = jnp.dot(
            masked(weights_ref[block, slot], slot, counts_ref[block]),
            padded[pl.ds(start, rows), :],
            preferred_element_type=jnp.float32,
        )
        total = part if total is None else total + part
    return total


def table_kernel(ids_ref, counts_ref, side_ref, weights_ref, own_ref, before_ref, after_ref, relayed_ref, out_ref, padded):
    edge, own_rows = before_ref.shape[0], own_ref.shape[0]
    padded[pl.ds(0, edge), :] = before_ref[...]
    padded[pl.ds(edge, own_rows), :] = own_ref[...]
    padded[pl.ds(edge + own_rows, edge), :] = after_ref[...]

    @pl.when(side_ref[0] == 1)
    def _():
        padded[pl.ds(0, edge), :] = relayed_ref[...]

    @pl.when(side_ref[0] == 2)
    def _():
        padded[pl.ds(edge + own_rows, edge), :] = relayed_ref[...]

    blocks, rows = weights_ref.shape[0], weights_ref.shape[2]
    for block in range(blocks):
        summed = blend_block(ids_ref, counts_ref, weights_ref, padded, block)
        out_ref[pl.ds(block * rows, rows), :] = summed.astype(out_ref.dtype)


def blend_table(ids, counts, weights, own, before, after, relayed, side, tile=512):
    rows, columns = own.shape
    edge = before.shape[0]
    tile = math.gcd(tile, columns)
    smem = pl.BlockSpec(memory_space=pltpu.SMEM)
    strip = lambda count: pl.BlockSpec((count, tile), lambda i: (0, i))
    new_rows = weights.shape[0] * weights.shape[2]
    return pl.pallas_call(
        table_kernel,
        grid=(columns // tile,),
        out_shape=jax.ShapeDtypeStruct((new_rows, columns), own.dtype),
        in_specs=[smem, smem, smem, pl.BlockSpec(weights.shape, lambda i: (0, 0, 0, 0)), strip(rows)] + [strip(edge)] * 3,
        out_specs=strip(new_rows),
        scratch_shapes=[pltpu.VMEM((rows + 2 * edge, tile), own.dtype)],
        compiler_params=pltpu.CompilerParams(vmem_limit_bytes=32 << 20),
        cost_estimate=pl.CostEstimate(
            flops=0, bytes_accessed=0, transcendentals=0
        ),
        name="blend_table",
    )(ids, counts, side, weights, own, before, after, relayed)


def stats_kernel(ids_ref, counts_ref, weights_ref, *refs):
    *source_refs, goals_ref, out_ref, padded, logits = refs
    start = 0
    for source_ref in source_refs:
        padded[pl.ds(start, source_ref.shape[0]), :] = source_ref[...]
        start += source_ref.shape[0]
    blocks, rows = weights_ref.shape[0], weights_ref.shape[2]
    tokens = padded.shape[1]
    goals = goals_ref[...]
    peak = jnp.full((1, tokens), -jnp.inf, jnp.float32)
    picked = jnp.zeros((1, tokens), jnp.float32)
    for block in range(blocks):
        summed = blend_block(ids_ref, counts_ref, weights_ref, padded, block)
        logits[pl.ds(block * rows, rows), :] = summed
        peak = jnp.maximum(peak, jnp.max(summed, axis=0, keepdims=True))
        row_ids = lax.broadcasted_iota(jnp.int32, summed.shape, 0) + block * rows
        picked = picked + jnp.sum(jnp.where(row_ids == goals, summed, 0.0), axis=0, keepdims=True)
    total = jnp.zeros((1, tokens), jnp.float32)
    for block in range(blocks):
        values = jnp.exp(logits[pl.ds(block * rows, rows), :] - peak)
        total = total + jnp.sum(values, axis=0, keepdims=True)
    out_ref[0:1, :] = peak
    out_ref[1:2, :] = total
    out_ref[2:3, :] = picked


def local_stats(ids, counts, weights, source, goals):
    tokens = source[0].shape[1]
    source_rows = sum(value.shape[0] for value in source)
    smem = pl.BlockSpec(memory_space=pltpu.SMEM)
    vmem = pl.BlockSpec(memory_space=pltpu.VMEM)
    new_rows = weights.shape[0] * weights.shape[2]
    return pl.pallas_call(
        stats_kernel,
        out_shape=jax.ShapeDtypeStruct((3, tokens), jnp.float32),
        in_specs=[smem, smem, vmem] + [vmem] * (len(source) + 1),
        out_specs=vmem,
        scratch_shapes=[
            pltpu.VMEM((source_rows, tokens), source[0].dtype),
            pltpu.VMEM((new_rows, tokens), jnp.float32),
        ],
        compiler_params=pltpu.CompilerParams(vmem_limit_bytes=32 << 20),
        cost_estimate=pl.CostEstimate(
            flops=2 * weights.size * tokens, bytes_accessed=2 * source_rows * tokens, transcendentals=new_rows * tokens
        ),
        name="blend_stats",
    )(ids, counts, weights, *source, goals)


def product_kernel(where_ref, *refs, pieces, chunks, bands, final):
    piece_refs, refs = refs[:pieces], refs[pieces:]
    chunk_refs, refs = refs[:chunks], refs[chunks:]
    carried_ref, refs = (refs[0], refs[1:]) if final else (None, refs)
    out_refs, (total, held, block, sems) = refs[:-4], refs[-4:]
    width = held.shape[2]
    rows_at = [sum(size for _, size in bands[:band]) for band in range(len(bands))]

    def copies(at, piece_ref):
        start = pl.multiple_of(where_ref[1, at] * width, width)
        for band, (first, size) in enumerate(bands):
            yield pltpu.make_async_copy(
                piece_ref.at[pl.ds(first, size), pl.ds(start, width)],
                held.at[at, pl.ds(rows_at[band], size), :],
                sems.at[1 + band, at],
            )

    def block_copy(at):
        return pltpu.make_async_copy(chunk_refs[at], block.at[at], sems.at[0, at])

    def carried_copies():
        for band, (first, size) in enumerate(bands):
            yield pltpu.make_async_copy(
                carried_ref.at[pl.ds(first, size), :], total.at[pl.ds(rows_at[band], size), :], sems.at[1 + band, chunks]
            )

    if final:
        for copy in carried_copies():
            copy.start()
    else:
        total[...] = jnp.zeros_like(total)
    for at in range(chunks):
        @pl.when(where_ref[2, at] == 1)
        def _(at=at):
            block_copy(at).start()

        for piece, piece_ref in enumerate(piece_refs):
            @pl.when((where_ref[2, at] == 1) & (where_ref[0, at] == piece))
            def _(at=at, piece_ref=piece_ref):
                for copy in copies(at, piece_ref):
                    copy.start()

    if final:
        for copy in carried_copies():
            copy.wait()
    for at in range(chunks):
        @pl.when(where_ref[2, at] == 1)
        def _(at=at):
            block_copy(at).wait()
            for copy in copies(at, piece_refs[0]):
                copy.wait()
            total[...] += lax.dot_general(held[at], block[at], CONTRACT_LAST, preferred_element_type=jnp.float32)

    for out_ref, row in zip(out_refs, rows_at):
        out_ref[...] = total[pl.ds(row, out_ref.shape[0]), :].astype(out_ref.dtype)


def add_products(where, pieces, chunks, bands, carried=None):
    tokens, width = chunks[0].shape
    rows = sum(size for _, size in bands)
    final = carried is not None
    vmem = pl.BlockSpec(memory_space=pltpu.VMEM)
    hbm = pl.BlockSpec(memory_space=pltpu.HBM)
    if final:
        shapes = [jax.ShapeDtypeStruct((size, tokens), jnp.bfloat16) for _, size in bands]
    else:
        shapes = [jax.ShapeDtypeStruct((rows, tokens), jnp.float32)]
    return pl.pallas_call(
        functools.partial(product_kernel, pieces=len(pieces), chunks=len(chunks), bands=bands, final=final),
        out_shape=shapes,
        in_specs=[pl.BlockSpec(memory_space=pltpu.SMEM)] + [hbm] * (len(pieces) + len(chunks) + final),
        out_specs=[vmem] * len(shapes),
        scratch_shapes=[
            pltpu.VMEM((rows, tokens), jnp.float32),
            pltpu.VMEM((len(chunks), rows, width), jnp.bfloat16),
            pltpu.VMEM((len(chunks), tokens, width), jnp.bfloat16),
            pltpu.SemaphoreType.DMA((1 + len(bands), len(chunks) + 1)),
        ],
        compiler_params=pltpu.CompilerParams(vmem_limit_bytes=(52 if final else 58) << 20),
        cost_estimate=pl.CostEstimate(flops=0, bytes_accessed=0, transcendentals=0),
        name="last_product" if final else "early_product",
    )(where, *pieces, *chunks, *([carried] if final else []))


def ring_order(count):
    return list(range(0, count, 2)) + list(range(count - 1, 0, -2))


def nothing(*refs):
    del refs


def fence(*values):
    hbm = pl.BlockSpec(memory_space=pl.ANY)
    return pl.pallas_call(
        nothing,
        out_shape=[jax.ShapeDtypeStruct(value.shape, value.dtype) for value in values],
        in_specs=[hbm] * len(values),
        out_specs=[hbm] * len(values),
        input_output_aliases={i: i for i in range(len(values))},
        name="fence",
    )(*values)


def shifted(value, pairs):
    return lax.ppermute(value, "vocab", pairs)


def merge_stats(stats, axis):
    count = lax.axis_size(axis)
    index = lax.axis_index(axis)
    low = 1
    while low < count:
        group = min(4, count // low)
        place = (index // low) % group
        got = [stats] + [lax.ppermute(stats, axis, xor_perm(count, low * mask)) for mask in range(1, group)]
        ordered = []
        for at in range(group):
            value = got[0]
            for mask in range(1, group):
                value = jnp.where((place ^ mask) == at, got[mask], value)
            ordered.append(value)
        peak = functools.reduce(jnp.maximum, [value[0] for value in ordered])
        total = sum(value[1] * jnp.exp(value[0] - peak) for value in ordered)
        stats = jnp.stack([peak, total, sum(value[2] for value in ordered)])
        low *= group
    return stats


def body(src_embed, src_head, block_ids, slot_counts, slot_weights, hidden, targets, byte_counts):
    block_rows = slot_weights.shape[2]
    rows, quarter = src_embed.shape
    new_rows = slot_weights.shape[0] * block_rows
    vocab_index = lax.axis_index("vocab")
    halo = REACH * block_rows
    last_local = rows // block_rows + 2 * REACH - 1
    local_ids = jnp.clip(block_ids - (vocab_index * (rows // block_rows) - REACH), 0, last_local)

    count = lax.axis_size("vocab")
    tok_index, tok_count = lax.axis_index("tok"), lax.axis_size("tok")
    up = [(i, i + 1) for i in range(count - 1)]
    down = [(j, i) for i, j in up]
    bottom_edge, top_edge = src_embed[rows - halo :], src_embed[:halo]
    far = tok_count // 2
    near_masks = [1 << bit for bit in reversed(range(far.bit_length() - 1))]
    width = hidden.shape[1]

    def to_far(value):
        return lax.ppermute(value, "tok", xor_perm(tok_count, far))

    def spread(held_pieces):
        for mask in near_masks:
            for held in list(held_pieces):
                held_pieces[held | mask] = lax.ppermute(held_pieces[held], "tok", xor_perm(tok_count, mask))
        return held_pieces

    def assembled(held_pieces, start, size):
        whole = jnp.zeros((size, tok_count * quarter), src_head.dtype)
        for held, entries in held_pieces.items():
            for offset, entry in entries:
                whole = lax.dynamic_update_slice(whole, entry, (offset - start, (tok_index ^ held) * quarter))
        return whole

    def product(head, arrivals):
        total = None
        for origin, value in arrivals:
            columns = lax.dynamic_slice_in_dim(head, origin * width, value.shape[1], axis=1)
            part = lax.dot_general(columns, value, CONTRACT_LAST, preferred_element_type=jnp.float32)
            total = part if total is None else total + part
        return total

    if count == 8 and tok_count == 4:
        order = ring_order(count)
        at = jnp.where(vocab_index % 2 == 0, vocab_index // 2, count - 1 - vocab_index // 2)
        ahead = [(order[i], order[(i + 1) % count]) for i in range(count)]
        behind = [(j, i) for i, j in ahead]

        def origin(offset):
            place = (at + offset) % count
            return jnp.where(place < count // 2, 2 * place, 2 * (count - 1 - place) + 1)

        aside_pairs = [(2, 3), (3, 2), (4, 5), (5, 4)]
        up_pairs = [(0, 1), (1, 2), (2, 3), (3, 4), (4, 6), (6, 7)]
        down_pairs = [(1, 0), (3, 1), (4, 3), (5, 4), (6, 5), (7, 6)]
        side = jnp.where(vocab_index == 5, 1, jnp.where(vocab_index == 2, 2, 0))
        def by_parity(even_pairs, odd_pairs):
            return [
                (i * tok_count + t, j * tok_count + t)
                for t in range(tok_count)
                for i, j in (odd_pairs if t % 2 else even_pairs)
            ]

        send_a = lambda value: lax.ppermute(value, ("vocab", "tok"), by_parity(ahead, behind))
        send_b = lambda value: lax.ppermute(value, ("vocab", "tok"), by_parity(behind, ahead))
        way = 1 - 2 * (tok_index % 2)
        a1, b1 = send_a(hidden), send_b(hidden)
        far_head = to_far(src_head)
        aside = shifted(jnp.where(vocab_index < 4, top_edge, bottom_edge), aside_pairs)
        near_head = spread({0: src_head})[1]
        a1, b1, near_head = fence(a1, b1, near_head)
        a2, b2 = send_a(a1), send_b(b1)
        table_before = shifted(jnp.where(vocab_index == 4, aside, bottom_edge), up_pairs)
        table_after = shifted(jnp.where(vocab_index == 3, aside, top_edge), down_pairs)
        a2, b2 = fence(a2, b2)
        a3, b3 = send_a(a2), send_b(b2)
        new_embed = blend_table(
            local_ids, slot_counts, slot_weights, src_embed, table_before, table_after, aside, side.reshape(1)
        )
        a3, b3, new_embed, far_head = fence(a3, b3, new_embed, far_head)
        a4 = send_a(a3)
        far_near_head = spread({far: far_head})[far | 1]
        pieces = [src_head, near_head, far_head, far_near_head]
        per = count // tok_count
        offsets = [0, -1, 1, -2, 2, -3, 3, 4]
        origins = jnp.stack([origin(way * offset) for offset in offsets]).astype(jnp.int32)
        piece_of = (origins // per) ^ tok_index
        late_piece = (piece_of == 3).astype(jnp.int32)
        wanted = jnp.concatenate([late_piece[:7], jnp.ones((1,), jnp.int32)])
        early_where = jnp.stack([piece_of, origins % per, 1 - late_piece])[:, :7]
        late_where = jnp.stack([piece_of, origins % per, wanted])
        blocks = [hidden, a1, b1, a2, b2, a3, b3]
        (early,) = add_products(early_where, pieces[:3], blocks, [(0, rows)])
        late = lambda bands: add_products(late_where, pieces, blocks + [a4], bands, early)
        top_logits, bottom_logits = late([(0, halo), (rows - halo, halo)])
        (middle_logits,) = late([(halo, rows - 2 * halo)])
        source_logits = [top_logits, middle_logits, bottom_logits]
    else:
        pieces = spread({0: src_head, far: to_far(src_head)})
        whole_head = assembled({held: [(0, piece)] for held, piece in pieces.items()}, 0, rows)
        whole_rows = lax.all_gather(hidden, "vocab", axis=1, tiled=True)
        total = product(whole_head, [(0, whole_rows)]).astype(jnp.bfloat16)
        source_logits = [total[:halo], total[halo : rows - halo], total[rows - halo :]]
        table_before, table_after = shifted(bottom_edge, up), shifted(top_edge, down)
        new_embed = blend_table(
            local_ids, slot_counts, slot_weights, src_embed, table_before, table_after, table_before, jnp.zeros((1,), jnp.int32)
        )
    after_rows = shifted(source_logits[0], down)
    before_rows = shifted(source_logits[-1], up)
    goals = (targets - vocab_index * new_rows)[None, :]
    stats = local_stats(local_ids, slot_counts, slot_weights, [before_rows] + list(source_logits) + [after_rows], goals)
    stats = merge_stats(stats, "vocab")
    log_total = stats[0] + jnp.log(stats[1])
    token_bpb = (log_total - stats[2]) / (jnp.float32(math.log(2.0)) * byte_counts.astype(jnp.float32))

    return (new_embed, token_bpb)


def solution(mesh):
    in_specs = (
        P("vocab", "tok"),
        P("vocab", "tok"),
        P("vocab", None),
        P("vocab"),
        P("vocab", None, None, None),
        P("tok", "vocab"),
        P("tok"),
        P("tok"),
    )
    out_specs = (P("vocab", "tok"), P("tok"))
    return jax.shard_map(body, mesh=mesh, in_specs=in_specs, out_specs=out_specs, check_vma=False)
```
